32 devices in a mesh: sec: 4 (over y, core), tp: 4 (over z), rq: 2 (over x).
Axes of the slice: x: 2, y: 2, z: 4, core: 2. Of those that a mesh axis runs over, the one named last changes fastest.
Arguments:
- tree_token_embed: bfloat16 [2, 16, 16, 8192], P(None, ('sec', 'rq')), as said below
- input_norm_gain: float32 [8192], replicated, may hold values from 0.25 to 1.75
- query_weight: bfloat16 [8192, 8192], P('rq', 'tp'), may hold values from -0.0625 to 0.0625
- key_value_weight: bfloat16 [8192, 2048], P('rq', 'tp'), may hold values from -0.1875 to 0.1875
- output_weight: bfloat16 [8192, 8192], P('tp', 'rq'), may hold values from -0.0625 to 0.0625
- join_feature_weight: bfloat16 [8192, 8192], P('rq', ('sec', 'tp')), may hold values from -0.046875 to 0.046875
- join_embed_weight: bfloat16 [8192, 8192], P('rq', ('sec', 'tp')), may hold values from -0.046875 to 0.046875
- key_value_cache: bfloat16 [16, 256, 2048], P(('sec', 'rq'), 'tp'), as said below
- extra_token_embed: bfloat16 [2, 16, 8192], P(None, ('sec', 'tp'), 'rq'), may hold values from -6 to 6
- ancestor_mask: int32 [2, 16, 16, 16], P(None, 'sec'), may hold values from 0 to 1, as said below
- context_length: int32 [16], P('sec'), may hold values from 32 to 256, as said below
- accepted_leaf: int32 [2, 16], P(None, 'sec'), may hold values from 0 to 15, as said below
Outputs:
- target_feat: bfloat16 [2, 16, 16, 8192], P(None, ('sec', 'tp'), None, 'rq')
- draft_feat: bfloat16 [2, 16, 6, 8192], P(None, 'rq', None, ('sec', 'tp'))
The draws below stay inside these ranges and needn't reach their ends.
Inputs may be any that keep to these rules, and one draw needn't show every extreme that they name: `tree_token_embed`: embeddings of the tree tokens. `key_value_cache`: cached keys, already rotated, and values of each request, laid out as 8 heads each holding a key then a value of 128 entries. ancestor_mask[k, r, n, m] is 1 exactly when m is n or an ancestor of n; node 0 is the root, a parent has a lower index than its child, and each tree has nodes at every depth from 0 to 5 and none deeper. `context_length`: some request holds exactly 256 cached tokens. `accepted_leaf`: the accepted node's depth is below 6; in every round some request accepts exactly 6 nodes.
All inputs are finite; a program needn't handle non-finite values.
Results may differ from the reference program's by a relative error of at most 0.02.
The reference program's roundings to bfloat16 on the way count: a program that leaves them out, or rounds other values in their place, can miss the bound.
Values may be sent and summed in bfloat16 or wider, within the bound.
No kernel may reach another device: no remote copies, remote signals or barrier semaphores. Data moves between devices by JAX's collectives and lax.ppermute only.
A program may use at most 128 MiB of HBM per device.

```python
import math
import jax
import jax.numpy as jnp
from jax import lax

MODEL_WIDTH = 8192
QUERY_HEADS = 64
KEY_VALUE_HEADS = 8
HEAD_SIZE = 128
TREE_NODES = 16
ACC_MAX = 6
ROUND_COUNT = 2
REQUEST_COUNT = 16
CONTEXT_TOKENS = 256


def draw_tree_token_embed(key, part):
    first_random_key, second_random_key, third_random_key = jax.random.split(key, 3)
    shape_all = (ROUND_COUNT, REQUEST_COUNT, TREE_NODES, MODEL_WIDTH)
    starting_values = jax.random.normal(first_random_key, shape_all, jnp.float32)
    row_scale = jnp.exp(jax.random.uniform(second_random_key, (ROUND_COUNT, REQUEST_COUNT, TREE_NODES, 1), jnp.float32, math.log(0.3), math.log(3.0)))
    column_scale = jnp.exp(jax.random.uniform(third_random_key, (MODEL_WIDTH,), jnp.float32, math.log(0.3), math.log(3.0)))
    return (starting_values * row_scale * column_scale).astype(jnp.bfloat16)


def draw_key_value_cache(key, part):
    first_random_key = jax.random.fold_in(key, 0)
    starting_values = jax.random.normal(first_random_key, (REQUEST_COUNT, CONTEXT_TOKENS, KEY_VALUE_HEADS, 2, HEAD_SIZE), jnp.float32)
    value_scale = jnp.array([1.0, 4.0], jnp.float32).reshape(1, 1, 1, 2, 1)
    scaled_rows = starting_values * value_scale
    return scaled_rows.reshape(REQUEST_COUNT, CONTEXT_TOKENS, KEY_VALUE_HEADS * 2 * HEAD_SIZE).astype(jnp.bfloat16)


def tree_shape(key):
    top_depth = ACC_MAX - 1
    tree_count = ROUND_COUNT * REQUEST_COUNT
    first_random_key, second_random_key = jax.random.split(jax.random.fold_in(key, 11))
    extra = jax.random.randint(first_random_key, (tree_count, TREE_NODES - 1 - top_depth), 1, top_depth + 1)
    forced = jnp.broadcast_to(jnp.arange(1, top_depth + 1), (tree_count, top_depth))
    depths = jnp.concatenate([jnp.zeros((tree_count, 1), jnp.int32), jnp.sort(jnp.concatenate([forced, extra], axis=1).astype(jnp.int32), axis=1)], axis=1)
    node_ids = jnp.arange(TREE_NODES)
    scores = jax.random.randint(second_random_key, (tree_count, TREE_NODES, TREE_NODES), 0, 1 << 20) * TREE_NODES + node_ids[None, None, :]
    candidate = depths[:, None, :] == depths[:, :, None] - 1
    parents = jnp.argmax(jnp.where(candidate, scores, -1), axis=-1)
    identity = jnp.broadcast_to((node_ids[:, None] == node_ids[None, :]).astype(jnp.int32), (tree_count, TREE_NODES, TREE_NODES))
    ancestry = identity
    index_full = jnp.broadcast_to(parents[:, :, None], (tree_count, TREE_NODES, TREE_NODES))
    for level in range(top_depth):
        ancestry = jnp.maximum(identity, jnp.take_along_axis(ancestry, index_full, axis=1))
    return (ancestry.reshape(ROUND_COUNT, REQUEST_COUNT, TREE_NODES, TREE_NODES), depths.reshape(ROUND_COUNT, REQUEST_COUNT, TREE_NODES))


def draw_ancestor_mask(key, part):
    return tree_shape(key)[0].astype(jnp.int32)


def draw_accepted_leaf(key, part):
    ancestry, depths = tree_shape(key)
    first_random_key, second_random_key, third_random_key = jax.random.split(jax.random.fold_in(key, 23), 3)
    lengths = jax.random.randint(first_random_key, (ROUND_COUNT, REQUEST_COUNT), 1, ACC_MAX + 1)
    lucky = jax.random.randint(second_random_key, (ROUND_COUNT, 1), 0, 8)
    lengths = jnp.where(jnp.arange(REQUEST_COUNT)[None, :] % 8 == lucky, ACC_MAX, lengths)
    scores = jax.random.randint(third_random_key, (ROUND_COUNT, REQUEST_COUNT, TREE_NODES), 0, 1 << 20) * TREE_NODES + jnp.arange(TREE_NODES)
    leaves = jnp.argmax(jnp.where(depths == lengths[..., None] - 1, scores, -1), axis=-1)
    return leaves.astype(jnp.int32)


def draw_context_length(key, part):
    first_random_key, second_random_key = jax.random.split(key)
    lengths = jax.random.randint(first_random_key, (REQUEST_COUNT,), CONTEXT_TOKENS // 8, CONTEXT_TOKENS + 1)
    chosen = jax.random.randint(second_random_key, (), 0, REQUEST_COUNT)
    return jnp.where(jnp.arange(REQUEST_COUNT) == chosen, CONTEXT_TOKENS, lengths).astype(jnp.int32)


def block_scale(rng, shape, cuts, smallest, high):
    factor_of, own = 1.0, jax.random.fold_in(rng, 6)
    for dim, shards_of in cuts:
        heights = jnp.exp(jax.random.uniform(jax.random.fold_in(own, dim), (shards_of,), jnp.float32, smallest / len(cuts), high / len(cuts)))
        factor_of = factor_of * jnp.repeat(heights, shape[dim] // shards_of).reshape([-1 if axis == dim else 1 for axis in range(len(shape))])
    return factor_of


def bell_draw(stream_key, dims, deviation, most, pieces=(), held_as=jnp.bfloat16):
    result = deviation * jax.random.normal(stream_key, dims, jnp.float32)
    if pieces:
        result = result * block_scale(stream_key, dims, pieces, -0.22, 0.18)
    return jnp.clip(result, -most, most).astype(held_as)


def setup_inputs(seed: int = 0) -> dict:
    splits = jax.random.split(jax.random.key(seed), 13)
    tree_token_embed = draw_tree_token_embed(jax.random.fold_in(splits[12], 71), 0)
    input_norm_gain = jnp.clip(1.0 + 0.15 * jax.random.normal(splits[1], (MODEL_WIDTH,), jnp.float32), 0.25, 1.75)
    query_weight = bell_draw(splits[2], (MODEL_WIDTH, QUERY_HEADS * HEAD_SIZE), MODEL_WIDTH ** -0.5, 0.0625, ((0, 2), (1, 4)))
    key_value_weight = bell_draw(splits[3], (MODEL_WIDTH, 2 * KEY_VALUE_HEADS * HEAD_SIZE), (MODEL_WIDTH // 8) ** -0.5, 0.1875, ((0, 2), (1, 4)))
    output_weight = bell_draw(splits[4], (QUERY_HEADS * HEAD_SIZE, MODEL_WIDTH), (QUERY_HEADS * HEAD_SIZE) ** -0.5, 0.0625, ((0, 4), (1, 2)))
    join_feature_weight = bell_draw(splits[5], (MODEL_WIDTH, MODEL_WIDTH), (2 * MODEL_WIDTH) ** -0.5, 0.046875, ((0, 2), (1, 16)))
    join_embed_weight = bell_draw(splits[6], (MODEL_WIDTH, MODEL_WIDTH), (2 * MODEL_WIDTH) ** -0.5, 0.046875, ((0, 2), (1, 16)))
    key_value_cache = draw_key_value_cache(jax.random.fold_in(splits[12], 71), 0)
    extra_token_embed = bell_draw(splits[8], (ROUND_COUNT, REQUEST_COUNT, MODEL_WIDTH), 1.0, 6.0, ((1, 16), (2, 2)))
    ancestor_mask = draw_ancestor_mask(jax.random.fold_in(splits[12], 71), 0)
    context_length = draw_context_length(jax.random.fold_in(splits[12], 71), 0)
    accepted_leaf = draw_accepted_leaf(jax.random.fold_in(splits[12], 71), 0)
    return {"tree_token_embed": tree_token_embed, "input_norm_gain": input_norm_gain, "query_weight": query_weight, "key_value_weight": key_value_weight, "output_weight": output_weight, "join_feature_weight": join_feature_weight, "join_embed_weight": join_embed_weight, "key_value_cache": key_value_cache, "extra_token_embed": extra_token_embed, "ancestor_mask": ancestor_mask, "context_length": context_length, "accepted_leaf": accepted_leaf}


NORM_EPSILON = 1e-05
ROPE_BASE = 500000.0
MASK_FLOOR = -1e+30

def rotary(values, position):
    half_width = values.shape[-1] // 2
    frequency = jnp.power(jnp.float32(ROPE_BASE), -jnp.arange(half_width).astype(jnp.float32) / half_width)
    angles = position.astype(jnp.float32)[..., None] * frequency
    cosine = jnp.cos(angles)
    sine_part = jnp.sin(angles)
    first_half = values[..., :half_width]
    second_half = values[..., half_width:]
    return jnp.concatenate([first_half * cosine - second_half * sine_part, second_half * cosine + first_half * sine_part], axis=-1)

def attend(request_item):
    query_rows, cached_rows, length, tree_key_rows, tree_value, tree_valid, cached_key_rows, cached_value_rows, old_valid = request_item
    query_group_size = QUERY_HEADS // KEY_VALUE_HEADS
    highest_precision = lax.Precision.HIGHEST
    scaling_factor = HEAD_SIZE ** (-0.5)
    grouped_queries = query_rows.astype(jnp.float32).reshape(TREE_NODES, KEY_VALUE_HEADS, query_group_size, HEAD_SIZE)
    cached_tokens = cached_rows.astype(jnp.float32).reshape(CONTEXT_TOKENS, KEY_VALUE_HEADS, 2, HEAD_SIZE)
    score_cache = jnp.einsum('nhgd,chd->hgnc', grouped_queries, cached_tokens[:, :, 0], precision=highest_precision) * scaling_factor
    tree_scores = jnp.einsum('izrf,ozf->zrio', grouped_queries, tree_key_rows, precision=highest_precision) * scaling_factor
    cached_scores = jnp.einsum('izrf,ozf->zrio', grouped_queries, cached_key_rows, precision=highest_precision) * scaling_factor
    valid_cache = jnp.broadcast_to((jnp.arange(CONTEXT_TOKENS) < length)[None, None, None, :], score_cache.shape)
    valid_tree = jnp.broadcast_to((tree_valid > 0)[None, None], tree_scores.shape)
    valid_old = jnp.broadcast_to((old_valid > 0)[None, None, None, :], cached_scores.shape)
    scores = jnp.concatenate([score_cache, tree_scores, cached_scores], axis=-1)
    usable = jnp.concatenate([valid_cache, valid_tree, valid_old], axis=-1)
    values_all = jnp.concatenate([cached_tokens[:, :, 1], tree_value.astype(jnp.float32), cached_value_rows.astype(jnp.float32)], axis=0)
    masked = jnp.where(usable, scores, MASK_FLOOR)
    peak_score = lax.optimization_barrier(jnp.max(masked, axis=-1, keepdims=True))
    weights = jnp.where(usable, jnp.exp(masked - peak_score), 0.0)
    total_weight = lax.optimization_barrier(jnp.sum(weights, axis=-1, keepdims=True))
    mixed = jnp.einsum('hgnc,chd->hgnd', weights, values_all, precision=highest_precision) / total_weight
    return jnp.transpose(mixed, (2, 0, 1, 3)).reshape(TREE_NODES, QUERY_HEADS * HEAD_SIZE).astype(jnp.bfloat16)

def reference(tree_token_embed, input_norm_gain, query_weight, key_value_weight, output_weight, join_feature_weight, join_embed_weight, key_value_cache, extra_token_embed, ancestor_mask, context_length, accepted_leaf):
    targets = []
    drafts = []
    cached_key_rows = jnp.zeros((REQUEST_COUNT, TREE_NODES, KEY_VALUE_HEADS, HEAD_SIZE), jnp.float32)
    cached_value_rows = jnp.zeros((REQUEST_COUNT, TREE_NODES, KEY_VALUE_HEADS, HEAD_SIZE), jnp.bfloat16)
    old_valid = jnp.zeros((REQUEST_COUNT, TREE_NODES), jnp.int32)
    offset = jnp.zeros((REQUEST_COUNT,), jnp.int32)
    slot_numbers = jnp.arange(ACC_MAX).astype(jnp.int32)
    node_ids = jnp.arange(TREE_NODES).astype(jnp.int32)
    for round_number in range(ROUND_COUNT):
        embedded_rows = tree_token_embed[round_number].astype(jnp.float32)
        inverse = lax.rsqrt(lax.optimization_barrier(jnp.mean(embedded_rows * embedded_rows, axis=-1, keepdims=True)) + NORM_EPSILON)
        normed_rows = (embedded_rows * inverse * input_norm_gain).astype(jnp.bfloat16).reshape(REQUEST_COUNT * TREE_NODES, MODEL_WIDTH)
        ancestry = ancestor_mask[round_number]
        depths = lax.optimization_barrier(jnp.sum(ancestry, axis=-1)) - 1
        position = context_length[:, None] + offset[:, None] + depths
        query_rows = jnp.dot(normed_rows, query_weight, preferred_element_type=jnp.float32).reshape(REQUEST_COUNT, TREE_NODES, QUERY_HEADS, HEAD_SIZE)
        query_rows = rotary(query_rows, position[..., None]).astype(jnp.bfloat16)
        key_value = jnp.dot(normed_rows, key_value_weight, preferred_element_type=jnp.float32).astype(jnp.bfloat16).reshape(REQUEST_COUNT, TREE_NODES, KEY_VALUE_HEADS, 2, HEAD_SIZE)
        tree_key_rows = rotary(key_value[:, :, :, 0].astype(jnp.float32), position[..., None])
        tree_value = key_value[:, :, :, 1]
        attended = lax.map(attend, (query_rows, key_value_cache, context_length, tree_key_rows, tree_value, ancestry, cached_key_rows, cached_value_rows, old_valid))
        mixed = jnp.dot(attended.reshape(REQUEST_COUNT * TREE_NODES, QUERY_HEADS * HEAD_SIZE), output_weight, preferred_element_type=jnp.float32).reshape(REQUEST_COUNT, TREE_NODES, MODEL_WIDTH)
        feature = (embedded_rows + mixed).astype(jnp.bfloat16)
        leaf_hot = (node_ids[None, :] == accepted_leaf[round_number][:, None]).astype(jnp.int32)
        on_path = lax.optimization_barrier(jnp.sum(leaf_hot[:, :, None] * ancestry, axis=1))
        accepted_nodes = lax.optimization_barrier(jnp.sum(on_path, axis=-1))
        pick_feat = (on_path[:, None, :] * (depths[:, None, :] == slot_numbers[None, :, None])).astype(jnp.float32)
        selected_embedding = (on_path[:, None, :] * (depths[:, None, :] == slot_numbers[None, :, None] + 1)).astype(jnp.float32)
        extra_token_on = (slot_numbers[None, :] == accepted_nodes[:, None] - 1).astype(jnp.float32)
        feat_slots = jnp.einsum('gtw,gwq->gtq', pick_feat, feature.astype(jnp.float32)).astype(jnp.bfloat16)
        embedding_slots = (jnp.einsum('gtw,gwq->gtq', selected_embedding, embedded_rows) + extra_token_on[:, :, None] * extra_token_embed[round_number].astype(jnp.float32)[:, None, :]).astype(jnp.bfloat16)
        drafted = jnp.dot(feat_slots.reshape(REQUEST_COUNT * ACC_MAX, MODEL_WIDTH), join_feature_weight, preferred_element_type=jnp.float32) + jnp.dot(embedding_slots.reshape(REQUEST_COUNT * ACC_MAX, MODEL_WIDTH), join_embed_weight, preferred_element_type=jnp.float32)
        drafts.append(drafted.astype(jnp.bfloat16).reshape(REQUEST_COUNT, ACC_MAX, MODEL_WIDTH))
        targets.append(feature)
        cached_key_rows = tree_key_rows
        cached_value_rows = tree_value
        old_valid = on_path
        offset = accepted_nodes
    return (jnp.stack(targets), jnp.stack(drafts))
```

```python
import functools

import jax
import jax.numpy as jnp
from jax import lax
from jax.experimental import pallas as pl
from jax.experimental.pallas import tpu as pltpu
from jax.sharding import PartitionSpec as P

QUERY_HEADS = 64
KEY_VALUE_HEADS = 8
HEAD_SIZE = 128
ACC_MAX = 6

NORM_EPSILON = 1e-05
ROPE_BASE = 500000.0
MASK_FLOOR = -1e30

BF = jnp.bfloat16
F32 = jnp.float32
VMEM = pl.BlockSpec(memory_space=pltpu.VMEM)
SMEM = pl.BlockSpec(memory_space=pltpu.SMEM)
GRANT = 14 << 20


def shift(count, step):
    return [(i, (i + step) % count) for i in range(count)]


def pick_part(parts, index):
    chosen = parts[0]
    for place in range(1, len(parts)):
        chosen = jnp.where(index == place, parts[place], chosen)
    return chosen


def after(values, *others):
    return lax.optimization_barrier((values, others))[0]


def dot(left, right):
    return jnp.dot(left, right, preferred_element_type=F32)


def in_vmem(array):
    return pltpu.with_memory_space_constraint(array, pltpu.VMEM)


def call(kernel, name, out_shape, operands, specs=None, scratch=()):
    return pl.pallas_call(
        kernel,
        out_shape=out_shape,
        in_specs=specs or [VMEM] * len(operands),
        out_specs=jax.tree.map(lambda _: VMEM, out_shape),
        scratch_shapes=list(scratch),
        compiler_params=pltpu.CompilerParams(vmem_limit_bytes=GRANT),
        name=name,
    )(*operands)


def tiles(total, most=512):
    step = min(total, most)
    return [pl.ds(at, step) for at in range(0, total, step)]


def project_kernel(raw_ref, inverse_ref, gain_ref, query_ref, key_value_ref, out_ref):
    inverse = inverse_ref[...]
    normed = jnp.concatenate(
        [
            (raw_ref[:, cut].astype(F32) * inverse * gain_ref[:, cut]).astype(BF)
            for cut in tiles(raw_ref.shape[1])
        ],
        axis=1,
    )
    for weight_ref, base in ((key_value_ref, query_ref.shape[1]), (query_ref, 0)):
        for cut in tiles(weight_ref.shape[1]):
            out_ref[:, pl.ds(base + cut.start, cut.size)] = dot(
                normed, weight_ref[:, cut]
            ).astype(out_ref.dtype)


def attention_kernel(n_q, n_kv, kv_base, dims, *refs):
    rounds, groups, nodes, kv_local, per_kv = dims
    q_refs, kv_refs = refs[:n_q], refs[n_q : n_q + n_kv]
    cos_ref, sin_ref = refs[n_q + n_kv : n_q + n_kv + 2]
    cache_refs = refs[n_q + n_kv + 2 : -3]
    cmask_ref, tmask_ref, out_ref = refs[-3:]
    cached = cmask_ref.shape[1]
    scaling = HEAD_SIZE ** (-0.5)
    half = HEAD_SIZE // 2
    contract_last = (((1,), (1,)), ((), ()))

    def total(parts, rows, cols):
        value = parts[0][rows, cols].astype(F32)
        for ref in parts[1:]:
            value = value + ref[rows, cols].astype(F32)
        return value

    def rot(value, rows):
        return value * cos_ref[rows, :] + pltpu.roll(value, half, 1) * sin_ref[rows, :]

    def row_slice(k, g):
        return pl.ds((k * groups + g) * nodes, nodes)

    def score(query, key):
        return lax.dot_general(query, key, contract_last, preferred_element_type=F32)

    def mix(weight, value):
        high = weight.astype(BF)
        low = (weight - high.astype(F32)).astype(BF)
        return dot(high, value) + dot(low, value)

    for g in range(groups):
        cached_ok = (
            jnp.broadcast_to(cmask_ref[g : g + 1, :], (per_kv * rounds * nodes, cached)) > 0
        )
        tree_ok = jnp.concatenate([tmask_ref[g]] * per_kv, axis=0) > 0
        for j in range(kv_local):
            key_cut = pl.ds(2 * j * HEAD_SIZE, HEAD_SIZE)
            value_cut = pl.ds((2 * j + 1) * HEAD_SIZE, HEAD_SIZE)
            keys, values = [], []
            for k in range(rounds):
                rows = row_slice(k, g)
                key = total(kv_refs, rows, pl.ds(kv_base + key_cut.start, HEAD_SIZE))
                value = total(kv_refs, rows, pl.ds(kv_base + value_cut.start, HEAD_SIZE))
                keys.append(rot(key.astype(BF).astype(F32), rows))
                values.append(value.astype(BF))
            tree_key = jnp.concatenate(keys, axis=0)
            tree_value = jnp.concatenate(values, axis=0)
            key_high = tree_key.astype(BF)
            key_low = (tree_key - key_high.astype(F32)).astype(BF)
            queries = []
            for h in range(per_kv):
                for k in range(rounds):
                    rows = row_slice(k, g)
                    query = total(q_refs, rows, pl.ds((j * per_kv + h) * HEAD_SIZE, HEAD_SIZE))
                    queries.append(rot(query, rows).astype(BF))
            query = jnp.concatenate(queries, axis=0)
            cache_key = jnp.concatenate([r[g, :, key_cut] for r in cache_refs], axis=0)
            cache_value = jnp.concatenate([r[g, :, value_cut] for r in cache_refs], axis=0)
            score_c = score(query, cache_key) * scaling
            score_t = (score(query, key_high) + score(query, key_low)) * scaling
            score_c = jnp.where(cached_ok, score_c, MASK_FLOOR)
            score_t = jnp.where(tree_ok, score_t, MASK_FLOOR)
            peak = jnp.maximum(
                jnp.max(score_c, axis=1, keepdims=True), jnp.max(score_t, axis=1, keepdims=True)
            )
            weight_c = jnp.where(cached_ok, jnp.exp(score_c - peak), 0.0)
            weight_t = jnp.where(tree_ok, jnp.exp(score_t - peak), 0.0)
            sums = jnp.sum(weight_c, axis=1, keepdims=True) + jnp.sum(
                weight_t, axis=1, keepdims=True
            )
            result = ((mix(weight_c, cache_value) + mix(weight_t, tree_value)) / sums).astype(BF)
            span = rounds * nodes
            for h in range(per_kv):
                out_ref[
                    pl.ds(g * span, span), pl.ds((j * per_kv + h) * HEAD_SIZE, HEAD_SIZE)
                ] = result[h * span : (h + 1) * span]


def output_kernel(n_parts, n_out, start_ref, *refs):
    parts, weight_ref = refs[:n_parts], refs[n_parts]
    outs, total_ref = refs[n_parts + 1 : n_parts + 1 + n_out], refs[-1]
    rows = outs[0].shape[0]
    source = jnp.concatenate([r[...] for r in parts], axis=0)
    for cut in tiles(weight_ref.shape[1]):
        total_ref[...] = dot(source, weight_ref[:, cut])
        for place, out in enumerate(outs):
            begin = pl.multiple_of(start_ref[place], rows)
            out[:, cut] = total_ref[pl.ds(begin, rows), :].astype(out.dtype)


def feature_kernel(n_parts, *refs):
    parts, (raw_ref, choose_ref, feature_ref, slots_ref) = refs[:n_parts], refs[n_parts:]
    chunks = choose_ref.shape[0]
    width = feature_ref.shape[1] // chunks
    slots = None
    for c in range(chunks):
        cut = pl.ds(c * width, width)
        mixed = parts[0][:, cut].astype(F32)
        for ref in parts[1:]:
            mixed = mixed + ref[:, cut].astype(F32)
        feature = (raw_ref[:, cut].astype(F32) + mixed).astype(BF)
        feature_ref[:, cut] = feature
        chosen = dot(choose_ref[c], feature)
        slots = chosen if slots is None else slots + chosen
    slots_ref[...] = slots.astype(BF)


def embed_kernel(raw_ref, extra_ref, choose_ref, extra_choose_ref, slots_ref):
    chunks = choose_ref.shape[0]
    width = raw_ref.shape[1] // chunks
    slots = None
    for c in range(chunks):
        cut = pl.ds(c * width, width)
        chosen = dot(choose_ref[c], raw_ref[:, cut]) + dot(extra_choose_ref[c], extra_ref[:, cut])
        slots = chosen if slots is None else slots + chosen
    slots_ref[...] = slots.astype(BF)


def join_kernel(n_pieces, n_out, added, *refs):
    pieces = refs[:n_pieces]
    id_ref, weight_ref = refs[n_pieces : n_pieces + 2]
    outs = refs[len(refs) - n_out :]
    chunks, inner = id_ref.shape
    width = weight_ref.shape[0] // chunks
    height = sum(out.shape[0] for out in outs)
    source = jnp.concatenate([r[...] for r in pieces], axis=0)
    wanted = lax.broadcasted_iota(jnp.int32, (height, inner), 0)
    total = refs[n_pieces + 2][...] if added else None
    for c in range(chunks):
        choose = (wanted == id_ref[c : c + 1, :]).astype(F32).astype(BF)
        rows = dot(choose, source).astype(BF)
        part = dot(rows, weight_ref[pl.ds(c * width, width), :])
        total = part if total is None else total + part
    size = height // n_out
    for place, out in enumerate(outs):
        out[...] = total[place * size : (place + 1) * size].astype(out.dtype)


def on_device(
    tree_token_embed,
    input_norm_gain,
    query_weight,
    key_value_weight,
    output_weight,
    join_feature_weight,
    join_embed_weight,
    key_value_cache,
    extra_token_embed,
    ancestor_mask,
    context_length,
    accepted_leaf,
):
    sec_n = lax.axis_size("sec")
    tp_n = lax.axis_size("tp")
    rq_n = lax.axis_size("rq")
    me_s = lax.axis_index("sec")
    me_t = lax.axis_index("tp")
    me_r = lax.axis_index("rq")
    rounds, groups, nodes, width = tree_token_embed.shape
    rows = rounds * groups * nodes
    half = query_weight.shape[0]
    sec_req = ancestor_mask.shape[1]
    block_req = sec_req // tp_n
    requests = sec_n * sec_req
    q_cols = query_weight.shape[1]
    kv_cols = key_value_weight.shape[1]
    heads_dev = q_cols // HEAD_SIZE
    per_group = QUERY_HEADS // KEY_VALUE_HEADS
    kv_local = max(1, heads_dev // per_group)
    per_kv = heads_dev // kv_local
    head_cols = 2 * HEAD_SIZE
    part_len = key_value_cache.shape[1]
    node_ids = jnp.arange(nodes)
    slots = jnp.arange(ACC_MAX)

    raw = tree_token_embed.reshape(rows, width)

    def columns(d):
        return lax.dynamic_slice_in_dim(raw, d * half, half, 1)

    raw_sent = [columns((me_r + s) % rq_n) for s in range(1, rq_n)]
    raw_others = [
        lax.ppermute(x, "rq", shift(rq_n, s)) for s, x in zip(range(1, rq_n), raw_sent)
    ]
    raw_late = after(raw, raw_sent)
    wide = raw_late.astype(F32)
    inverse = lax.rsqrt(jnp.mean(wide * wide, axis=-1, keepdims=True) + NORM_EPSILON)
    inverse_others = [lax.ppermute(inverse, "rq", shift(rq_n, s)) for s in range(1, rq_n)]

    cache_late = after(key_value_cache, inverse)

    def head_block(d):
        start = (d * heads_dev) // per_group * head_cols
        return lax.dynamic_slice_in_dim(cache_late, start, kv_local * head_cols, 2)

    cache_parts = [head_block(me_t)] + [
        lax.ppermute(head_block((me_t + u) % tp_n), "tp", shift(tp_n, u)) for u in range(1, tp_n)
    ]
    sources = (me_t - jnp.arange(tp_n)) % tp_n
    cache_position = (sources[:, None] * part_len + jnp.arange(part_len)[None, :]).reshape(-1)

    gain = lax.dynamic_slice_in_dim(input_norm_gain, me_r * half, half, 0)[None, :]
    query_held, key_value_held = in_vmem(query_weight), in_vmem(key_value_weight)
    raw_own = lax.dynamic_slice_in_dim(raw_late, me_r * half, half, 1)

    def project(part, scale, dtype):
        return call(
            project_kernel,
            "project",
            jax.ShapeDtypeStruct((rows, q_cols + kv_cols), dtype),
            (part, scale, gain, query_held, key_value_held),
        )

    own_partial = project(raw_own, inverse, F32)

    own_start = me_r * groups
    ctx_own = lax.dynamic_slice_in_dim(context_length, own_start, groups, 0)
    depths = jnp.sum(ancestor_mask, axis=-1) - 1
    leaf_hot = (node_ids[None, None, :] == accepted_leaf[:, :, None]).astype(jnp.int32)
    path = jnp.sum(leaf_hot[:, :, :, None] * ancestor_mask, axis=2)
    accepted = jnp.sum(path, axis=-1)
    mask_own = lax.dynamic_slice_in_dim(ancestor_mask, own_start, groups, 1)
    depth_own = lax.dynamic_slice_in_dim(depths, own_start, groups, 1)
    path_own = lax.dynamic_slice_in_dim(path, own_start, groups, 1)
    accepted_own = lax.dynamic_slice_in_dim(accepted, own_start, groups, 1)
    offsets, offset = [], jnp.zeros((groups,), jnp.int32)
    for k in range(rounds):
        offsets.append(offset)
        offset = accepted_own[k]
    position = (ctx_own[None, :] + jnp.stack(offsets))[:, :, None] + depth_own
    turn = HEAD_SIZE // 2
    frequency = jnp.power(F32(ROPE_BASE), -jnp.arange(turn).astype(F32) / turn)
    angles = position.astype(F32).reshape(rows, 1) * frequency
    cosine, sine = jnp.cos(angles), jnp.sin(angles)
    cos_full = jnp.concatenate([cosine, cosine], axis=-1)
    sin_full = jnp.concatenate([-sine, sine], axis=-1)
    cache_ok = (cache_position[None, :] < ctx_own[:, None]).astype(F32)
    tree_rows = []
    for k in range(rounds):
        parts = []
        for m in range(rounds):
            if m == k:
                parts.append(mask_own[k])
            elif m == k - 1:
                parts.append(jnp.broadcast_to(path_own[m][:, None, :], mask_own[k].shape))
            else:
                parts.append(jnp.zeros_like(mask_own[k]))
        tree_rows.append(jnp.concatenate(parts, axis=-1))
    tree_ok = jnp.concatenate(tree_rows, axis=1).astype(F32)

    block_start = me_t * block_req
    tree_count = block_req * rounds
    slot_rows = tree_count * ACC_MAX
    chunks = 4
    span = half // chunks

    def of_trees(value):
        return jnp.swapaxes(lax.dynamic_slice_in_dim(value, block_start, block_req, 1), 0, 1)

    depth_block, path_block = of_trees(depths), of_trees(path)
    accepted_block = of_trees(accepted[..., None])
    level = depth_block[:, :, None, :]
    on_path = path_block[:, :, None, :] > 0
    same = jnp.eye(tree_count, dtype=jnp.bool_)
    stacked = jnp.eye(chunks, dtype=jnp.bool_)

    def chooser(match):
        flat = match.reshape(tree_count, ACC_MAX, 1, -1) & same[:, None, :, None]
        flat = flat.reshape(slot_rows, -1)
        full = stacked[:, :, None, None] & flat[None, None]
        return full.reshape(chunks, chunks * slot_rows, -1).astype(BF)

    choose_feat = chooser(on_path & (level == slots[:, None]))
    choose_embed = chooser(on_path & (level == slots[:, None] + 1))
    choose_extra = chooser((slots == accepted_block - 1)[..., None])

    flips = [0]
    bit = sec_n // 2
    while bit:
        flips = flips + [f ^ bit for f in flips]
        bit //= 2
    held_req = requests // rq_n
    source_sec = me_s ^ jnp.array(flips, jnp.int32)
    request = (source_sec[:, None] * sec_req + sources[None, :] * block_req)[
        :, :, None
    ] + jnp.arange(block_req)
    half_of = (request // held_req - me_r) % rq_n
    row_of = half_of * (rounds * held_req) + request % held_req
    row_id = (
        (row_of[..., None] + jnp.arange(rounds) * held_req)[..., None] * ACC_MAX + slots
    ).reshape(sec_n * tp_n, slot_rows)
    row_ids = jnp.where(
        stacked[:, None, :, None], row_id[None, :, None, :], -1
    ).reshape(chunks, -1)

    raw_others, inverse_others = after((raw_others, inverse_others), own_partial)
    q_parts = [own_partial]
    sent = []
    for s, part, scale in zip(range(1, rq_n), raw_others, inverse_others):
        sent.append(project(part, scale, BF))
        q_parts.append(lax.ppermute(sent[-1], "rq", shift(rq_n, -s)))

    source_step = (me_r - block_start // groups) % rq_n

    def tree_of(part):
        block = lax.dynamic_slice_in_dim(
            part.reshape(rounds, groups, nodes, half), block_start % groups, block_req, 1
        )
        return jnp.swapaxes(block, 0, 1).reshape(tree_count * nodes, half)

    late_parts = after([raw_own] + list(raw_others), sent)
    raw_block = pick_part([tree_of(p) for p in late_parts], source_step)
    slot_shape = jax.ShapeDtypeStruct((chunks * slot_rows, span), BF)

    def gather_slots(block):
        pieces = [block] + [lax.ppermute(block, "tp", shift(tp_n, u)) for u in range(1, tp_n)]
        bit = sec_n // 2
        while bit:
            perm = [(i, i ^ bit) for i in range(sec_n)]
            pieces = pieces + [lax.ppermute(x, "sec", perm) for x in pieces]
            bit //= 2
        return pieces

    extra_rows = jnp.swapaxes(extra_token_embed, 0, 1).reshape(tree_count, half)
    embed_pieces = gather_slots(
        call(
            embed_kernel, "embed", slot_shape, (raw_block, extra_rows, choose_embed, choose_extra)
        )
    )
    out_width = join_embed_weight.shape[1]
    draft_rows = rounds * requests * ACC_MAX
    embed_joined = call(
        functools.partial(join_kernel, len(embed_pieces), 1, False),
        "join_embed",
        jax.ShapeDtypeStruct((draft_rows, out_width), F32),
        (*embed_pieces, row_ids, in_vmem(join_embed_weight)),
    )

    kv_parts, kv_base = q_parts, q_cols
    if kv_cols < head_cols:
        summed = sum((p[:, q_cols:].astype(F32) for p in q_parts[1:]), q_parts[0][:, q_cols:])
        everyone = lax.all_gather(summed.astype(BF), "tp", axis=1, tiled=True)
        start = (me_t * heads_dev) // per_group * head_cols
        kv_parts, kv_base = [lax.dynamic_slice_in_dim(everyone, start, head_cols, 1)], 0
    n_q = len(q_parts)
    dims = (rounds, groups, nodes, kv_local, per_kv)
    attended = call(
        functools.partial(attention_kernel, n_q, len(kv_parts), kv_base, dims),
        "attend",
        jax.ShapeDtypeStruct((rows, q_cols), BF),
        (*q_parts, *kv_parts, cos_full, sin_full, *cache_parts, cache_ok, tree_ok),
    )

    attended_parts = [attended] + [
        lax.ppermute(attended, "rq", shift(rq_n, s)) for s in range(1, rq_n)
    ]
    block_rows = tree_count * nodes
    per_rq = groups // block_req
    goal = (me_t + jnp.arange(tp_n)) % tp_n
    starts = ((me_r - goal // per_rq) % rq_n) * rows + (goal % per_rq) * block_rows
    blocks = call(
        functools.partial(output_kernel, rq_n, tp_n),
        "output",
        [
            jax.ShapeDtypeStruct((block_rows, half), F32 if u == 0 else BF)
            for u in range(tp_n)
        ],
        (starts.astype(jnp.int32), *attended_parts, in_vmem(output_weight)),
        [SMEM] + [VMEM] * (rq_n + 1),
        [pltpu.VMEM((rq_n * rows, min(512, half)), F32)],
    )
    mixed_parts = [blocks[0]] + [
        lax.ppermute(blocks[u], "tp", shift(tp_n, u)) for u in range(1, tp_n)
    ]
    feature, feat_slots = call(
        functools.partial(feature_kernel, tp_n),
        "feature",
        [jax.ShapeDtypeStruct((block_rows, half), BF), slot_shape],
        (*mixed_parts, raw_block, choose_feat),
    )

    feat_pieces = gather_slots(feat_slots)
    joined = call(
        functools.partial(join_kernel, len(feat_pieces), rq_n, True),
        "join_feature",
        [
            jax.ShapeDtypeStruct((draft_rows // rq_n, out_width), F32 if s == 0 else BF)
            for s in range(rq_n)
        ],
        (*feat_pieces, row_ids, in_vmem(join_feature_weight), embed_joined),
    )
    drafted = joined[0]
    for s in range(1, rq_n):
        drafted = drafted + lax.ppermute(joined[s], "rq", shift(rq_n, s)).astype(F32)
    draft = drafted.astype(BF).reshape(rounds, held_req, ACC_MAX, out_width)
    target = jnp.swapaxes(feature.reshape(block_req, rounds, nodes, half), 0, 1)
    return target, draft


def solution(mesh):
    placed = (
        P(None, ("sec", "rq"), None, None),
        P(),
        P("rq", "tp"),
        P("rq", "tp"),
        P("tp", "rq"),
        P("rq", ("sec", "tp")),
        P("rq", ("sec", "tp")),
        P(("sec", "rq"), "tp", None),
        P(None, ("sec", "tp"), "rq"),
        P(None, "sec", None, None),
        P("sec"),
        P(None, "sec"),
    )
    return jax.shard_map(
        on_device,
        mesh=mesh,
        in_specs=placed,
        out_specs=(P(None, ("sec", "tp"), None, "rq"), P(None, "rq", None, ("sec", "tp"))),
        check_vma=False,
    )
```
